256 devices in a mesh: pair: 4 (over y), virt: 16 (over x, z_hi), slab: 4 (over z_lo, core).
Axes of the slice: x: 4, y: 4, z: 8 (z_hi: 4, z_lo: 2; z = z_hi * 2 + z_lo), core: 2. Of those that a mesh axis runs over, the one named last changes fastest.
Arguments:
- amplitudes: float32 [2048, 4, 2048], P('pair', 'slab', 'virt'), may hold values from -6 to 6
- integrals: float32 [4, 2048, 24576], P('slab', None, 'virt'), may hold values from -0.1875 to 0.1875
- pair_irrep: int32 [16], P('pair'), may hold values from 0 to 7, as said below
- cd_irrep: int32 [4, 16], replicated, may hold values from 0 to 7
- residual_tile_irrep: int32 [192], P('virt'), may hold values from 0 to 7, as said below
- partner: int32 [2048], replicated, may hold values from 0 to 2047, as said below
Outputs:
- residual: float32 [2048, 24576], P(('pair', 'slab'), 'virt')
The draws below stay inside these ranges and needn't reach their ends.
Inputs may be any that keep to these rules, and one draw needn't show every extreme that they name: partner is an involution without fixed points: partner[partner[r]] = r and partner[r] != r. `pair_irrep`: every irrep of an occupied-pair tile is also the irrep of some contracted tile. `residual_tile_irrep`: every irrep of a residual tile is also the irrep of some contracted tile.
All inputs are finite; a program needn't handle non-finite values.
Results may differ from the reference program's by a relative error of at most 0.0001.
Values sent between devices are 32-bit elements; how exact they have to be, the bound alone decides.
A program may use at most 128 MiB of HBM per device.

```python
import jax
import jax.numpy as jnp
from jax import lax

PAIR_TILE_SIZE = 128
CDK = 2048
PAIRS = 2048
AB = 24576
N_SLAB = 4


def draw_partner(key, part):
    order = jax.random.permutation(jax.random.fold_in(key, 7), PAIRS).astype(jnp.int32)
    firsts = order[0::2]
    seconds = order[1::2]
    result = jnp.zeros((PAIRS,), jnp.int32)
    result = result.at[firsts].set(seconds)
    result = result.at[seconds].set(firsts)
    return result


def irrep_offset(key):
    return jax.random.randint(jax.random.fold_in(key, 11), (), 0, 8).astype(jnp.int32)


def irrep_span():
    return min(8, N_SLAB * (CDK // PAIR_TILE_SIZE))


def draw_cd_irrep(key, part):
    offset = irrep_offset(key)
    tiles = N_SLAB * (CDK // PAIR_TILE_SIZE)
    order = jax.random.permutation(jax.random.fold_in(key, 14), tiles).astype(jnp.int32)
    return ((offset + order) % 8).reshape(N_SLAB, CDK // PAIR_TILE_SIZE).astype(jnp.int32)


def draw_pair_irrep(key, part):
    offset = irrep_offset(key)
    count = PAIRS // PAIR_TILE_SIZE
    picks = jax.random.randint(jax.random.fold_in(key, 12), (count,), 0, irrep_span()).astype(jnp.int32)
    values = (offset + picks) % 8
    return values.at[0].set(offset).astype(jnp.int32)


def draw_residual_tile_irrep(key, part):
    offset = irrep_offset(key)
    count = AB // PAIR_TILE_SIZE
    picks = jax.random.randint(jax.random.fold_in(key, 13), (count,), 0, irrep_span()).astype(jnp.int32)
    values = (offset + picks) % 8
    return values.at[0].set(offset).astype(jnp.int32)


def level_of(own_key, dims, cuts, smallest, high):
    gain = 1.0
    for axis_at, blocks in cuts:
        steps = jax.random.uniform(jax.random.fold_in(jax.random.fold_in(own_key, 6), axis_at), (blocks,), jnp.float32, smallest / len(cuts), high / len(cuts))
        gain = gain * jnp.repeat(jnp.exp(steps), dims[axis_at] // blocks).reshape((-1,) + (1,) * (len(dims) - 1 - axis_at))
    return gain


def scatter_about(key, dims, deviation, bound, split=(), kind=jnp.bfloat16):
    values = deviation * jax.random.normal(key, dims, jnp.float32)
    if split:
        values = values * level_of(key, dims, split, -0.22, 0.18)
    return jnp.clip(values, -bound, bound).astype(kind)


def setup_inputs(seed: int = 0) -> dict:
    key_list = jax.random.split(jax.random.key(seed), 7)
    return {
        "amplitudes": scatter_about(key_list[0], (PAIRS, N_SLAB, CDK), 1.0, 6.0, ((0, 4), (1, 4), (2, 16)), jnp.float32),
        "integrals": scatter_about(key_list[1], (N_SLAB, CDK, AB), (N_SLAB * CDK // 8) ** -0.5, 0.1875, ((0, 4), (2, 16)), jnp.float32),
        "pair_irrep": draw_pair_irrep(jax.random.fold_in(key_list[6], 71), 0),
        "cd_irrep": draw_cd_irrep(jax.random.fold_in(key_list[6], 71), 0),
        "residual_tile_irrep": draw_residual_tile_irrep(jax.random.fold_in(key_list[6], 71), 0),
        "partner": draw_partner(jax.random.fold_in(key_list[6], 71), 0),
    }


def flip_halves(values):
    row_count, col_count = values.shape
    return values.reshape(row_count, col_count // 128, 2, 64)[:, :, ::-1, :].reshape(row_count, col_count)


def reference(amplitudes, integrals, pair_irrep, cd_irrep, residual_tile_irrep, partner):
    row_irr = jnp.repeat(pair_irrep, PAIR_TILE_SIZE)
    residual_pair_tiles = residual_tile_irrep.shape[0]
    ladder = jnp.zeros((amplitudes.shape[0], integrals.shape[2]), jnp.float32)
    for current_slab_index in range(N_SLAB):
        integral_pair_row = cd_irrep[current_slab_index]
        cd_cols = jnp.repeat(integral_pair_row, PAIR_TILE_SIZE)
        masked_t = amplitudes[:, current_slab_index, :] * (row_irr[:, None] == cd_cols[None, :]).astype(jnp.float32)
        irrep_match_mask = (integral_pair_row[:, None] == residual_tile_irrep[None, :]).astype(jnp.float32)
        integral_pair_tiles = integral_pair_row.shape[0]
        symmetry_masked_integrals = (integrals[current_slab_index].reshape(integral_pair_tiles, PAIR_TILE_SIZE, residual_pair_tiles, PAIR_TILE_SIZE) * irrep_match_mask[:, None, :, None]).reshape(integral_pair_tiles * PAIR_TILE_SIZE, residual_pair_tiles * PAIR_TILE_SIZE)
        ladder = ladder + jnp.dot(masked_t, symmetry_masked_integrals, precision=lax.Precision.HIGHEST, preferred_element_type=jnp.float32)
    partner_rows = jnp.take(ladder, partner, axis=0)
    return ladder + flip_halves(partner_rows)
```

```python
import functools

import jax
import jax.numpy as jnp
from jax import lax
from jax.experimental import pallas as pl
from jax.experimental.pallas import tpu as pltpu
from jax.sharding import PartitionSpec as P

MESH = pl.DeviceIdType.MESH
VMEM = pltpu.VMEM
SMEM = pltpu.SMEM
F32 = jnp.float32
BF16 = jnp.bfloat16
W_FAST = 6
CAP_FAST = 32
VLIM = 64 * 1024 * 1024 - 128 * 1024


def vspec():
    return pl.BlockSpec(memory_space=VMEM)


def sspec():
    return pl.BlockSpec(memory_space=SMEM)


def split2(x):
    hi = x.astype(BF16)
    return hi, (x - hi.astype(F32)).astype(BF16)


def split3(x):
    hi = x.astype(BF16)
    rest = x - hi.astype(F32)
    mid = rest.astype(BF16)
    return hi, mid, (rest - mid.astype(F32)).astype(BF16)


def dot(a, b):
    return jnp.dot(a, b, preferred_element_type=F32)


def pick(onehot, x):
    hi, mid, lo = split3(x)
    return dot(onehot, hi) + dot(onehot, mid) + dot(onehot, lo)


def tile_iota(dim, shape=(8, 128)):
    return lax.broadcasted_iota(jnp.int32, shape, dim)


def gather_kernel(n_pair, slots, meta, *refs):
    if meta:
        (pi, cd, ri, amp, part, t0, t1, rank, irr, branch, ybuf, ssem, rsem, ysend, yrecv) = refs
    else:
        (pi, cd, amp, t0, t1, ssem, rsem) = refs
    p = lax.axis_index("pair")
    v = lax.axis_index("virt")
    s = lax.axis_index("slab")
    x, zh = v // 4, v % 4

    def at(dx, dz):
        return ((x + dx) % 4) * 4 + (zh + dz) % 4

    barrier = pltpu.get_barrier_semaphore()
    near = [(1, 0), (3, 0), (0, 1), (0, 3)]
    for dx, dz in near:
        pl.semaphore_signal(barrier, inc=1, device_id={"virt": at(dx, dz)}, device_id_type=MESH)
    peers = len(near)
    if meta:
        for d in range(1, n_pair):
            pl.semaphore_signal(
                barrier, inc=1, device_id={"pair": (p + d) % n_pair}, device_id_type=MESH
            )
        peers += max(n_pair - 1, 0)

    mine = cd[s, v]
    count = jnp.int32(0)
    index = [jnp.int32(0), jnp.int32(0)]
    for r in range(4):
        hit = pi[r] == mine
        for t in range(2):
            index[t] = jnp.where(hit & (count == slots[t]), r, index[t])
        count = count + jnp.where(hit, 1, 0)
    t0[v, 0:128, :] = amp[index[0]]
    t1[v, 0:128, :] = amp[index[1]]

    lane = tile_iota(1)
    if meta:
        own = jnp.full((8, 128), -1.0, F32)
        for q in range(12):
            own = jnp.where(lane == q, ri[q].astype(F32), own)
        t0[v, 128:136, :] = own
        repeat = jnp.int32(0)
        for r in range(4):
            same = jnp.int32(0)
            for r2 in range(4):
                same = same + jnp.where(pi[r] == pi[r2], 1, 0)
            repeat = jnp.maximum(repeat, same)
        row = jnp.where(lane == 16 + p, repeat.astype(F32), jnp.zeros((8, 128), F32))
        for r in range(4):
            row = jnp.where(lane == 4 * p + r, pi[r].astype(F32), row)
        ybuf[p] = row

    pl.semaphore_wait(barrier, peers)

    started = []

    def send(dx, dz, t, hx, hz):
        buf = (t0, t1)[t]
        src = at(-dx, -dz)
        k_here = (dx * 4 + dz) * 2 + t
        k_there = (((dx + hx) % 4) * 4 + (dz + hz) % 4) * 2 + t
        way = {(1, 0): 0, (-1, 0): 1, (0, 1): 2, (0, -1): 3}[(hx, hz)]
        copy = pltpu.make_async_remote_copy(
            src_ref=buf.at[src],
            dst_ref=buf.at[src],
            send_sem=ssem.at[k_here * 4 + way],
            recv_sem=rsem.at[k_there],
            device_id={"virt": at(hx, hz)},
            device_id_type=MESH,
        )
        copy.start()
        started.append(copy)

    def arrive(dx, dz, t):
        buf = (t0, t1)[t]
        dst = buf.at[at(-dx, -dz)]
        pltpu.make_async_copy(dst, dst, rsem.at[(dx * 4 + dz) * 2 + t]).wait()

    def both(dz, t):
        send(0, dz, t, 1, 0)
        send(0, dz, t, -1, 0)

    send(0, 0, 0, 1, 0)
    send(0, 0, 1, -1, 0)
    send(0, 0, 0, 0, 1)
    send(0, 0, 1, 0, -1)
    send(0, 0, 1, 1, 0)
    send(0, 0, 0, -1, 0)
    send(0, 0, 1, 0, 1)
    send(0, 0, 0, 0, -1)
    ycopies = []
    if meta:
        for d in range(1, n_pair):
            copy = pltpu.make_async_remote_copy(
                src_ref=ybuf.at[p],
                dst_ref=ybuf.at[p],
                send_sem=ysend.at[d - 1],
                recv_sem=yrecv.at[d - 1],
                device_id={"pair": (p + d) % n_pair},
                device_id_type=MESH,
            )
            copy.start()
            ycopies.append(copy)
        dest = part[...] // 256
        upper = (tile_iota(0, (128, 128)) < tile_iota(1, (128, 128))).astype(F32).astype(BF16)
        total = jnp.zeros((16, 128), F32)
        most = jnp.zeros((16, 1), F32)
        for d in range(8):
            hot = (dest == d).astype(F32)
            total = total + hot * dot(hot.astype(BF16), upper)
            most = jnp.maximum(most, jnp.sum(hot, axis=1, keepdims=True))
        rank[...] = total.astype(jnp.int32)
        crowd = jnp.max(most)

    arrive(1, 0, 0)
    send(1, 0, 0, 1, 0)
    arrive(3, 0, 1)
    send(3, 0, 1, -1, 0)
    arrive(0, 1, 0)
    send(0, 1, 0, 0, 1)
    both(1, 0)
    arrive(0, 3, 1)
    send(0, 3, 1, 0, -1)
    both(3, 1)
    arrive(0, 1, 1)
    both(1, 1)
    arrive(0, 3, 0)
    both(3, 0)
    arrive(1, 1, 0)
    send(1, 1, 0, 1, 0)
    arrive(3, 3, 1)
    send(3, 3, 1, -1, 0)
    arrive(0, 2, 0)
    both(2, 0)
    arrive(0, 2, 1)
    both(2, 1)
    arrive(3, 1, 1)
    send(3, 1, 1, -1, 0)
    arrive(1, 3, 0)
    send(1, 3, 0, 1, 0)
    arrive(1, 2, 0)
    send(1, 2, 0, 1, 0)
    arrive(3, 2, 1)
    send(3, 2, 1, -1, 0)
    done = {(1, 0, 0), (3, 0, 1), (1, 1, 0), (3, 3, 1), (3, 1, 1), (1, 3, 0), (1, 2, 0), (3, 2, 1)}
    for dx in (1, 3, 2):
        for dz in range(4):
            for t in range(2):
                if (dx, dz, t) not in done:
                    arrive(dx, dz, t)
    for copy in started:
        copy.wait_send()
    if meta:
        for copy in ycopies:
            copy.wait()
        table = ybuf[0]
        for q in range(1, n_pair):
            table = table + ybuf[q]
        irr[...] = table
        again = jnp.max(jnp.where((lane >= 16) & (lane < 16 + n_pair), table, 0.0))
        tags = t0[:, 128, :]
        wide = jnp.zeros((16, 1), F32)
        for k in range(8):
            hits = jnp.sum((tags == float(k)).astype(F32), axis=1, keepdims=True)
            wide = jnp.maximum(wide, hits)
        widest = jnp.max(wide)
        full = (widest > float(W_FAST)) | (crowd > float(CAP_FAST))
        more = again > 2.0
        branch[0] = jnp.where(full, 2, jnp.where(more, 1, 0)).astype(jnp.int32)


def gather(n_pair, slots, meta, cid, pi, cd, ri, amp, part):
    rows0 = 136 if meta else 128
    outs = [
        jax.ShapeDtypeStruct((16, rows0, 128), F32),
        jax.ShapeDtypeStruct((16, 128, 128), F32),
    ]
    out_specs = [vspec(), vspec()]
    scratch = [pltpu.SemaphoreType.DMA((128,)), pltpu.SemaphoreType.DMA((32,))]
    if meta:
        args, in_specs = (pi, cd, ri, amp, part), [sspec(), sspec(), sspec(), vspec(), vspec()]
        outs += [
            jax.ShapeDtypeStruct((16, 128), jnp.int32),
            jax.ShapeDtypeStruct((8, 128), F32),
            jax.ShapeDtypeStruct((1,), jnp.int32),
        ]
        out_specs += [vspec(), vspec(), sspec()]
        scratch = (
            [pltpu.VMEM((n_pair, 8, 128), F32)]
            + scratch
            + [pltpu.SemaphoreType.DMA((3,)), pltpu.SemaphoreType.DMA((3,))]
        )
    else:
        args, in_specs = (pi, cd, amp), [sspec(), sspec(), vspec()]
    return pl.pallas_call(
        functools.partial(gather_kernel, n_pair, slots, meta),
        out_shape=outs,
        in_specs=in_specs,
        out_specs=out_specs,
        scratch_shapes=scratch,
        compiler_params=pltpu.CompilerParams(
            collective_id=cid, has_side_effects=True, vmem_limit_bytes=32 * 1024 * 1024
        ),
        name=f"gather{cid}",
    )(*args)


def multiply_kernel(width, n_t, *refs):
    pi, cd, ri = refs[:3]
    v_hbm = refs[3]
    tiles = refs[4 : 4 + n_t]
    out = refs[4 + n_t]
    vbuf, clist, qlist, sem = refs[5 + n_t :]
    s = lax.axis_index("slab")

    def block(c, q):
        rows = pl.ds(pl.multiple_of(c * 128, 128), 128)
        cols = pl.ds(pl.multiple_of(q * 128, 128), 128)
        return rows, cols

    def wanted(c):
        k = cd[s, c]
        return (pi[0] == k) | (pi[1] == k) | (pi[2] == k) | (pi[3] == k)

    def fetch(c, n):
        k = cd[s, c]

        def one(q, n):
            hit = ri[q] == k

            @pl.when(hit)
            def _():
                rows, cols = block(c, q)
                pltpu.make_async_copy(v_hbm.at[rows, cols], vbuf.at[rows, cols], sem).start()

            return n + jnp.where(hit, 1, 0)

        return lax.cond(wanted(c), lambda n: lax.fori_loop(0, 12, one, n), lambda n: n, n)

    total = lax.fori_loop(0, 16, fetch, jnp.int32(0))

    counts = []
    for r in range(4):
        k = pi[r]

        def note_c(c, n, r=r, k=k):
            @pl.when(cd[s, c] == k)
            def _():
                clist[r, n] = c

            return n + jnp.where(cd[s, c] == k, 1, 0)

        def note_q(q, n, r=r, k=k):
            @pl.when(ri[q] == k)
            def _():
                qlist[r, n] = q

            return n + jnp.where(ri[q] == k, 1, 0)

        n_c = lax.fori_loop(0, 16, note_c, jnp.int32(0))
        n_q = lax.fori_loop(0, 12, note_q, jnp.int32(0))
        turn = jnp.int32(0)
        for r2 in range(r):
            turn = turn + jnp.where(pi[r2] == k, 1, 0)
        counts.append((n_c, n_q, turn))

    def drain(i, carry):
        rows, cols = block(0, 0)
        pltpu.make_async_copy(v_hbm.at[rows, cols], vbuf.at[rows, cols], sem).wait()
        return carry

    lax.fori_loop(0, total, drain, 0)

    for r in range(4):
        n_c, n_q, turn = counts[r]
        for j in range(width):

            @pl.when(j < n_q)
            def _(r=r, j=j, n_c=n_c, turn=turn):
                q = qlist[r, j]

                def step(i, acc):
                    c = clist[r, i]
                    left = tiles[0][c, 0:128, :]
                    for t in range(1, n_t):
                        left = jnp.where(turn == t, tiles[t][c, 0:128, :], left)
                    rows, cols = block(c, q)
                    a_hi, a_lo = split2(left)
                    b_hi, b_lo = split2(vbuf[rows, cols])
                    return acc + (dot(a_hi, b_hi) + (dot(a_hi, b_lo) + dot(a_lo, b_hi)))

                out[r, j] = lax.fori_loop(0, n_c, step, jnp.zeros((128, 128), F32))

            @pl.when(j >= n_q)
            def _(r=r, j=j):
                out[r, j] = jnp.zeros((128, 128), F32)


def multiply(width, pi, cd, ri, v, tiles):
    n_t = len(tiles)
    return pl.pallas_call(
        functools.partial(multiply_kernel, width, n_t),
        out_shape=jax.ShapeDtypeStruct((4, width, 128, 128), F32),
        in_specs=[sspec()] * 3 + [pl.BlockSpec(memory_space=pl.ANY)] + [vspec()] * n_t,
        out_specs=vspec(),
        scratch_shapes=[
            pltpu.VMEM((2048, 1536), F32),
            pltpu.SMEM((4, 16), jnp.int32),
            pltpu.SMEM((4, 12), jnp.int32),
            pltpu.SemaphoreType.DMA,
        ],
        compiler_params=pltpu.CompilerParams(vmem_limit_bytes=32 * 1024 * 1024),
        name=f"multiply{width}_{n_t}",
    )(pi, cd, ri, v, *tiles)


def combine_kernel(n_pair, width, cap, *refs):
    (pi, ri, part, part_t, rank, irr, pp, out) = refs[:8]
    (b1, far, b2, lad, pack, rows, yrow) = refs[8:15]
    (s1, r1, s1n, r1n, s2, r2, s3, r3, s4, r4) = refs[15:]
    p = lax.axis_index("pair")
    s = lax.axis_index("slab")
    z, core = s // 2, s % 2
    sib = z * 2 + (1 - core)
    over = (1 - z) * 2 + core
    n_chip = 2 * n_pair
    chip = p * 2 + z
    tile = p * 4 + s

    def chip_at(d):
        other = (chip + d) % n_chip
        return other, {"pair": other // 2, "slab": (other % 2) * 2 + core}

    barrier = pltpu.get_barrier_semaphore()
    pl.semaphore_signal(barrier, inc=1, device_id={"slab": sib}, device_id_type=MESH)
    for d in range(1, n_chip):
        pl.semaphore_signal(barrier, inc=1, device_id=chip_at(d)[1], device_id_type=MESH)
    pl.semaphore_wait(barrier, n_chip)

    def remote(src, dst, ssem, rsem, device):
        return pltpu.make_async_remote_copy(
            src_ref=src,
            dst_ref=dst,
            send_sem=ssem,
            recv_sem=rsem,
            device_id=device,
            device_id_type=MESH,
        )

    first = []
    for j in range(width):
        copy = remote(
            pp.at[(1 - z) * 2 + (1 - core), j], b1.at[0, j], s1.at[j], r1.at[j], {"slab": sib}
        )
        copy.start()
        first.append(copy)
    home = remote(pp.at[sib], b1.at[1], s1n, r1n, {"slab": sib})
    home.start()
    second = []
    for j in range(width):
        first[j].wait_recv()
        far[j] = pp[over, j] + b1[0, j]
        copy = remote(far.at[j], b2.at[j], s2.at[j], r2.at[j], {"slab": over})
        copy.start()
        second.append(copy)

    key = part[pl.ds(tile, 1), :] // 256 * cap + rank[pl.ds(tile, 1), :]
    slot = lax.broadcasted_iota(jnp.int32, (n_chip * cap, 128), 0)
    send_hot = (slot == key).astype(F32).astype(BF16)
    lane16 = lax.broadcasted_iota(jnp.int32, (128, 16), 1)
    mate = jnp.sum(jnp.where(lane16 == tile, part_t[...], 0), axis=1, keepdims=True)
    mate_tile, mate_row = mate // 128, mate % 128
    lane = lax.broadcasted_iota(jnp.int32, (128, 128), 1)
    low_hot = (lane == mate_row).astype(F32).astype(BF16)
    ranks = lax.dot_general(
        low_hot,
        rank[...].astype(F32).astype(BF16),
        (((1,), (1,)), ((), ())),
        preferred_element_type=F32,
    )
    mate_hot = lane16 == mate_tile
    mate_rank = jnp.sum(jnp.where(mate_hot, ranks, 0.0), axis=1, keepdims=True).astype(jnp.int32)
    mate_irrep = jnp.sum(
        jnp.where(lane == mate_tile, jnp.broadcast_to(irr[0:1, :], (128, 128)), 0.0),
        axis=1,
        keepdims=True,
    )
    source = (mate_tile % 2) * (n_chip * cap) + (mate_tile // 2) * cap + mate_rank
    arrive_hot = (
        (lax.broadcasted_iota(jnp.int32, (128, 2 * n_chip * cap), 1) == source)
        .astype(F32)
        .astype(BF16)
    )

    home.wait_recv()
    for j in range(width):
        second[j].wait_recv()
        lad[j] = pp[s, j] + b1[1, j] + b2[j]
    for j in range(width):
        cols = slice(j * 128, (j + 1) * 128)
        packed = pick(send_hot, lad[j])
        for c in range(n_chip):
            pack[c, :, cols] = packed[c * cap : (c + 1) * cap]

    third = []
    for d in (list(range(1, n_chip))):
        other, device = chip_at(d)
        copy = remote(pack.at[other], rows.at[core, chip], s3.at[d], r3.at[d], device)
        copy.start()
        third.append((d, copy))
    rows[core, chip] = pack[chip]
    fourth = []

    def relay(d):
        from_chip = (chip - d) % n_chip
        block = rows.at[core, from_chip]
        copy = remote(block, block, s4.at[d], r4.at[d], {"slab": sib})
        copy.start()
        fourth.append((d, copy))

    relay(0)
    order = sorted(third, key=lambda e: min(e[0], n_chip - e[0]))
    for d, copy in order:
        copy.wait_recv()
        relay(d)
    for d, copy in fourth:
        copy.wait_recv()
    for j in range(width):
        cols = slice(j * 128, (j + 1) * 128)
        got = jnp.concatenate(
            [rows[c, d, :, cols] for c in range(2) for d in range(n_chip)], axis=0
        )
        yrow[j] = pick(arrive_hot, got)

    own = pi[s]
    for q in range(12):
        k = ri[q]
        at = jnp.int32(0)
        for q2 in range(q):
            at = at + jnp.where(ri[q2] == k, 1, 0)
        at = jnp.minimum(at, width - 1)
        direct = jnp.where(own == k, lad[at], 0.0)
        swapped = jnp.where(mate_irrep == k.astype(F32), yrow[at], 0.0)
        out[:, q * 128 : (q + 1) * 128] = direct + pltpu.roll(swapped, 64, 1)
    for copy in first + [home] + second:
        copy.wait_send()
    for _, copy in third + fourth:
        copy.wait_send()


def combine(n_pair, width, cap, cid, pi, ri, part, part_t, rank, irr, pp):
    n_chip = 2 * n_pair
    dma = pltpu.SemaphoreType.DMA
    return pl.pallas_call(
        functools.partial(combine_kernel, n_pair, width, cap),
        out_shape=jax.ShapeDtypeStruct((128, 1536), F32),
        in_specs=[sspec(), sspec()] + [vspec()] * 5,
        out_specs=vspec(),
        scratch_shapes=[
            pltpu.VMEM((2, width, 128, 128), F32),
            pltpu.VMEM((width, 128, 128), F32),
            pltpu.VMEM((width, 128, 128), F32),
            pltpu.VMEM((width, 128, 128), F32),
            pltpu.VMEM((n_chip, cap, width * 128), F32),
            pltpu.VMEM((2, n_chip, cap, width * 128), F32),
            pltpu.VMEM((width, 128, 128), F32),
            dma((width,)),
            dma((width,)),
            dma,
            dma,
            dma((width,)),
            dma((width,)),
            dma((n_chip,)),
            dma((n_chip,)),
            dma((n_chip,)),
            dma((n_chip,)),
        ],
        compiler_params=pltpu.CompilerParams(
            collective_id=cid,
            has_side_effects=True,
            vmem_limit_bytes=VLIM if cap > CAP_FAST else 24 * 1024 * 1024,
        ),
        name=f"combine{cid}",
    )(pi, ri, part, part_t, rank, irr, pp)


def shards(n_pair, amplitudes, integrals, pi, cd, ri, partner):
    amp = amplitudes.reshape(4, 128, 128)
    v = integrals.reshape(integrals.shape[1:])
    part = partner.reshape(16, 128)
    part_t = part.T
    t0, t1, rank, irr, branch = gather(n_pair, (0, 1), True, 0, pi, cd, ri, amp, part)

    def rest(width, cap, cid, extra, t0, t1):
        tiles = [t0, t1]
        if extra is not None:
            tiles += gather(n_pair, (2, 3), False, extra, pi, cd, ri, amp, part)
        pp = multiply(width, pi, cd, ri, v, tiles)
        return combine(n_pair, width, cap, cid, pi, ri, part, part_t, rank, irr, pp)

    return lax.switch(
        branch[0],
        [
            functools.partial(rest, W_FAST, CAP_FAST, 1, None),
            functools.partial(rest, W_FAST, CAP_FAST, 2, 3),
            functools.partial(rest, 12, 128, 4, 5),
        ],
        t0,
        t1,
    )


def solution(mesh):
    placed = (P("pair", "slab", "virt"), P("slab", None, "virt"), P("pair"), P(), P("virt"), P())
    return jax.shard_map(
        functools.partial(shards, mesh.shape["pair"]),
        mesh=mesh,
        in_specs=placed,
        out_specs=P(("pair", "slab"), "virt"),
        check_vma=False,
    )
```

```python
import functools

import jax
import jax.numpy as jnp
from jax import lax
from jax.experimental import pallas as pl
from jax.experimental.pallas import tpu as pltpu
from jax.sharding import PartitionSpec as P

MESH = pl.DeviceIdType.MESH
VMEM = pltpu.VMEM
SMEM = pltpu.SMEM
F32 = jnp.float32
BF16 = jnp.bfloat16
W_FAST = 5
W_MORE = 6
CAP_FAST = 32
VLIM = 64 * 1024 * 1024 - 128 * 1024


def vspec():
    return pl.BlockSpec(memory_space=VMEM)


def sspec():
    return pl.BlockSpec(memory_space=SMEM)


def split2(x):
    hi = x.astype(BF16)
    return hi, (x - hi.astype(F32)).astype(BF16)


def split3(x):
    hi = x.astype(BF16)
    rest = x - hi.astype(F32)
    mid = rest.astype(BF16)
    return hi, mid, (rest - mid.astype(F32)).astype(BF16)


def dot(a, b):
    return jnp.dot(a, b, preferred_element_type=F32)


def pick(onehot, x):
    hi, mid, lo = split3(x)
    return dot(onehot, hi) + dot(onehot, mid) + dot(onehot, lo)


def tile_iota(dim, shape=(8, 128)):
    return lax.broadcasted_iota(jnp.int32, shape, dim)


def gather_kernel(n_pair, slots, meta, *refs):
    if meta:
        (pi, cd, ri, amp, part, t0, t1, rank, irr, branch, ybuf, ssem, rsem, ysend, yrecv) = refs
    else:
        (pi, cd, amp, t0, t1, ssem, rsem) = refs
    p = lax.axis_index("pair")
    v = lax.axis_index("virt")
    s = lax.axis_index("slab")
    x, zh = v // 4, v % 4

    def at(dx, dz):
        return ((x + dx) % 4) * 4 + (zh + dz) % 4

    barrier = pltpu.get_barrier_semaphore()
    near = [(1, 0), (3, 0), (0, 1), (0, 3)]
    for dx, dz in near:
        pl.semaphore_signal(barrier, inc=1, device_id={"virt": at(dx, dz)}, device_id_type=MESH)
    peers = len(near)
    if meta:
        for d in range(1, n_pair):
            pl.semaphore_signal(
                barrier, inc=1, device_id={"pair": (p + d) % n_pair}, device_id_type=MESH
            )
        peers += max(n_pair - 1, 0)

    mine = cd[s, v]
    count = jnp.int32(0)
    index = [jnp.int32(0), jnp.int32(0)]
    for r in range(4):
        hit = pi[r] == mine
        for t in range(2):
            index[t] = jnp.where(hit & (count == slots[t]), r, index[t])
        count = count + jnp.where(hit, 1, 0)
    t0[v, 0:128, :] = amp[index[0]]
    t1[v, 0:128, :] = amp[index[1]]

    lane = tile_iota(1)
    if meta:
        own = jnp.full((8, 128), -1.0, F32)
        for q in range(12):
            own = jnp.where(lane == q, ri[q].astype(F32), own)
        t0[v, 128:136, :] = own
        repeat = jnp.int32(0)
        for r in range(4):
            same = jnp.int32(0)
            for r2 in range(4):
                same = same + jnp.where(pi[r] == pi[r2], 1, 0)
            repeat = jnp.maximum(repeat, same)
        row = jnp.where(lane == 16 + p, repeat.astype(F32), jnp.zeros((8, 128), F32))
        for r in range(4):
            row = jnp.where(lane == 4 * p + r, pi[r].astype(F32), row)
        ybuf[p] = row

    pl.semaphore_wait(barrier, peers)

    started = []

    def send(dx, dz, t, hx, hz):
        buf = (t0, t1)[t]
        src = at(-dx, -dz)
        k_here = (dx * 4 + dz) * 2 + t
        k_there = (((dx + hx) % 4) * 4 + (dz + hz) % 4) * 2 + t
        way = {(1, 0): 0, (-1, 0): 1, (0, 1): 2, (0, -1): 3}[(hx, hz)]
        copy = pltpu.make_async_remote_copy(
            src_ref=buf.at[src],
            dst_ref=buf.at[src],
            send_sem=ssem.at[k_here * 4 + way],
            recv_sem=rsem.at[k_there],
            device_id={"virt": at(hx, hz)},
            device_id_type=MESH,
        )
        copy.start()
        started.append(copy)

    def arrive(dx, dz, t):
        buf = (t0, t1)[t]
        dst = buf.at[at(-dx, -dz)]
        pltpu.make_async_copy(dst, dst, rsem.at[(dx * 4 + dz) * 2 + t]).wait()

    def both(dz, t):
        send(0, dz, t, 1, 0)
        send(0, dz, t, -1, 0)

    send(0, 0, 0, 1, 0)
    send(0, 0, 1, -1, 0)
    send(0, 0, 0, 0, 1)
    send(0, 0, 1, 0, -1)
    send(0, 0, 1, 1, 0)
    send(0, 0, 0, -1, 0)
    send(0, 0, 1, 0, 1)
    send(0, 0, 0, 0, -1)
    ycopies = []
    if meta:
        for d in range(1, n_pair):
            copy = pltpu.make_async_remote_copy(
                src_ref=ybuf.at[p],
                dst_ref=ybuf.at[p],
                send_sem=ysend.at[d - 1],
                recv_sem=yrecv.at[d - 1],
                device_id={"pair": (p + d) % n_pair},
                device_id_type=MESH,
            )
            copy.start()
            ycopies.append(copy)
        dest = part[...] // 256
        upper = (tile_iota(0, (128, 128)) < tile_iota(1, (128, 128))).astype(F32).astype(BF16)
        total = jnp.zeros((16, 128), F32)
        most = jnp.zeros((16, 1), F32)
        for d in range(8):
            hot = (dest == d).astype(F32)
            total = total + hot * dot(hot.astype(BF16), upper)
            most = jnp.maximum(most, jnp.sum(hot, axis=1, keepdims=True))
        rank[...] = total.astype(jnp.int32)
        crowd = jnp.max(most)

    arrive(1, 0, 0)
    send(1, 0, 0, 1, 0)
    arrive(3, 0, 1)
    send(3, 0, 1, -1, 0)
    arrive(0, 1, 0)
    send(0, 1, 0, 0, 1)
    both(1, 0)
    arrive(0, 3, 1)
    send(0, 3, 1, 0, -1)
    both(3, 1)
    arrive(0, 1, 1)
    both(1, 1)
    arrive(0, 3, 0)
    both(3, 0)
    arrive(1, 1, 0)
    send(1, 1, 0, 1, 0)
    arrive(3, 3, 1)
    send(3, 3, 1, -1, 0)
    arrive(0, 2, 0)
    both(2, 0)
    arrive(0, 2, 1)
    both(2, 1)
    arrive(3, 1, 1)
    send(3, 1, 1, -1, 0)
    arrive(1, 3, 0)
    send(1, 3, 0, 1, 0)
    arrive(1, 2, 0)
    send(1, 2, 0, 1, 0)
    arrive(3, 2, 1)
    send(3, 2, 1, -1, 0)
    done = {(1, 0, 0), (3, 0, 1), (1, 1, 0), (3, 3, 1), (3, 1, 1), (1, 3, 0), (1, 2, 0), (3, 2, 1)}
    for dx in (1, 3, 2):
        for dz in range(4):
            for t in range(2):
                if (dx, dz, t) not in done:
                    arrive(dx, dz, t)
    for copy in started:
        copy.wait_send()
    if meta:
        for copy in ycopies:
            copy.wait()
        table = ybuf[0]
        for q in range(1, n_pair):
            table = table + ybuf[q]
        irr[...] = table
        again = jnp.max(jnp.where((lane >= 16) & (lane < 16 + n_pair), table, 0.0))
        tags = t0[:, 128, :]
        wide = jnp.zeros((16, 1), F32)
        for k in range(8):
            hits = jnp.sum((tags == float(k)).astype(F32), axis=1, keepdims=True)
            wide = jnp.maximum(wide, hits)
        widest = jnp.max(wide)
        full = (widest > float(W_MORE)) | (crowd > float(CAP_FAST))
        step = jnp.where(again > 2.0, 2, jnp.where(widest > float(W_FAST), 1, 0))
        branch[0] = jnp.where(full, 3, step).astype(jnp.int32)


def gather(n_pair, slots, meta, cid, pi, cd, ri, amp, part):
    rows0 = 136 if meta else 128
    outs = [
        jax.ShapeDtypeStruct((16, rows0, 128), F32),
        jax.ShapeDtypeStruct((16, 128, 128), F32),
    ]
    out_specs = [vspec(), vspec()]
    scratch = [pltpu.SemaphoreType.DMA((128,)), pltpu.SemaphoreType.DMA((32,))]
    if meta:
        args, in_specs = (pi, cd, ri, amp, part), [sspec(), sspec(), sspec(), vspec(), vspec()]
        outs += [
            jax.ShapeDtypeStruct((16, 128), jnp.int32),
            jax.ShapeDtypeStruct((8, 128), F32),
            jax.ShapeDtypeStruct((1,), jnp.int32),
        ]
        out_specs += [vspec(), vspec(), sspec()]
        scratch = (
            [pltpu.VMEM((n_pair, 8, 128), F32)]
            + scratch
            + [pltpu.SemaphoreType.DMA((3,)), pltpu.SemaphoreType.DMA((3,))]
        )
    else:
        args, in_specs = (pi, cd, amp), [sspec(), sspec(), vspec()]
    return pl.pallas_call(
        functools.partial(gather_kernel, n_pair, slots, meta),
        out_shape=outs,
        in_specs=in_specs,
        out_specs=out_specs,
        scratch_shapes=scratch,
        compiler_params=pltpu.CompilerParams(
            collective_id=cid, has_side_effects=True, vmem_limit_bytes=8 * 1024 * 1024
        ),
        name=f"gather{cid}",
    )(*args)


def multiply_kernel(width, n_t, *refs):
    pi, cd, ri = refs[:3]
    v_hbm = refs[3]
    tiles = refs[4 : 4 + n_t]
    out = refs[4 + n_t]
    vbuf, clist, qlist, sem = refs[5 + n_t :]
    s = lax.axis_index("slab")

    def block(c, q):
        rows = pl.ds(pl.multiple_of(c * 128, 128), 128)
        cols = pl.ds(pl.multiple_of(q * 128, 128), 128)
        return rows, cols

    def wanted(c):
        k = cd[s, c]
        return (pi[0] == k) | (pi[1] == k) | (pi[2] == k) | (pi[3] == k)

    def fetch(c, n):
        k = cd[s, c]

        def one(q, n):
            hit = ri[q] == k

            @pl.when(hit)
            def _():
                rows, cols = block(c, q)
                pltpu.make_async_copy(v_hbm.at[rows, cols], vbuf.at[rows, cols], sem).start()

            return n + jnp.where(hit, 1, 0)

        return lax.cond(wanted(c), lambda n: lax.fori_loop(0, 12, one, n), lambda n: n, n)

    total = lax.fori_loop(0, 16, fetch, jnp.int32(0))

    counts = []
    for r in range(4):
        k = pi[r]

        def note_c(c, n, r=r, k=k):
            @pl.when(cd[s, c] == k)
            def _():
                clist[r, n] = c

            return n + jnp.where(cd[s, c] == k, 1, 0)

        def note_q(q, n, r=r, k=k):
            @pl.when(ri[q] == k)
            def _():
                qlist[r, n] = q

            return n + jnp.where(ri[q] == k, 1, 0)

        for j in range(12):
            qlist[r, j] = 0
        n_c = lax.fori_loop(0, 16, note_c, jnp.int32(0))
        n_q = lax.fori_loop(0, 12, note_q, jnp.int32(0))
        turn = jnp.int32(0)
        for r2 in range(r):
            turn = turn + jnp.where(pi[r2] == k, 1, 0)
        counts.append((n_c, n_q, turn))

    def drain(i, carry):
        rows, cols = block(0, 0)
        pltpu.make_async_copy(v_hbm.at[rows, cols], vbuf.at[rows, cols], sem).wait()
        return carry

    lax.fori_loop(0, total, drain, 0)

    for r in range(4):
        n_c, n_q, turn = counts[r]
        out[r] = jnp.zeros((width, 128, 128), F32)

        def step(i, carry, r=r, n_q=n_q, turn=turn):
            c = clist[r, i]
            left = tiles[0][c, 0:128, :]
            for t in range(1, n_t):
                left = jnp.where(turn == t, tiles[t][c, 0:128, :], left)
            a_hi, a_lo = split2(left)
            a3 = jnp.concatenate([a_hi, a_lo, a_hi], axis=1)
            for j in range(0, width, 2):

                @pl.when(j < n_q)
                def _(j=j):
                    rows, cols0 = block(c, qlist[r, j])
                    rows, cols1 = block(c, qlist[r, j + 1])
                    b = jnp.concatenate([vbuf[rows, cols0], vbuf[rows, cols1]], axis=1)
                    b_hi, b_lo = split2(b)
                    res = dot(a3, jnp.concatenate([b_hi, b_hi, b_lo], axis=0))
                    out[r, j] += res[:, 0:128]
                    if j + 1 == width:
                        return

                    @pl.when(j + 1 < n_q)
                    def _():
                        out[r, j + 1] += res[:, 128:256]

            return carry

        lax.fori_loop(0, n_c, step, 0)


def multiply(width, pi, cd, ri, v, tiles):
    n_t = len(tiles)
    return pl.pallas_call(
        functools.partial(multiply_kernel, width, n_t),
        out_shape=jax.ShapeDtypeStruct((4, width, 128, 128), F32),
        in_specs=[sspec()] * 3 + [pl.BlockSpec(memory_space=pl.ANY)] + [vspec()] * n_t,
        out_specs=vspec(),
        scratch_shapes=[
            pltpu.VMEM((2048, 1536), F32),
            pltpu.SMEM((4, 16), jnp.int32),
            pltpu.SMEM((4, 12), jnp.int32),
            pltpu.SemaphoreType.DMA,
        ],
        compiler_params=pltpu.CompilerParams(vmem_limit_bytes=20 * 1024 * 1024),
        name=f"multiply{width}_{n_t}",
    )(pi, cd, ri, v, *tiles)


def combine_kernel(n_pair, width, cap, chunks, *refs):
    (part, part_t, rank, irr, pp, lad, yrow, mate_out) = refs[:8]
    (b1, far, b2) = refs[8:11]
    n_chunk = len(chunks)
    packs, refs = refs[11 : 11 + n_chunk], refs[11 + n_chunk :]
    rows, refs = refs[:n_chunk], refs[n_chunk:]
    (s1, r1, s1n, r1n, s2, r2, s3, r3, s4, r4) = refs
    p = lax.axis_index("pair")
    s = lax.axis_index("slab")
    z, core = s // 2, s % 2
    sib = z * 2 + (1 - core)
    over = (1 - z) * 2 + core
    n_chip = 2 * n_pair
    chip = p * 2 + z
    tile = p * 4 + s

    def chip_at(d):
        other = (chip + d) % n_chip
        return other, {"pair": other // 2, "slab": (other % 2) * 2 + core}

    barrier = pltpu.get_barrier_semaphore()
    pl.semaphore_signal(barrier, inc=1, device_id={"slab": sib}, device_id_type=MESH)
    for d in range(1, n_chip):
        pl.semaphore_signal(barrier, inc=1, device_id=chip_at(d)[1], device_id_type=MESH)
    pl.semaphore_wait(barrier, n_chip)

    def remote(src, dst, ssem, rsem, device):
        return pltpu.make_async_remote_copy(
            src_ref=src,
            dst_ref=dst,
            send_sem=ssem,
            recv_sem=rsem,
            device_id=device,
            device_id_type=MESH,
        )

    first = []
    for j in range(width):
        copy = remote(
            pp.at[(1 - z) * 2 + (1 - core), j], b1.at[0, j], s1.at[j], r1.at[j], {"slab": sib}
        )
        copy.start()
        first.append(copy)
    home = remote(pp.at[sib], b1.at[1], s1n, r1n, {"slab": sib})
    home.start()
    second = []
    for j in range(width):
        first[j].wait_recv()
        far[j] = pp[over, j] + b1[0, j]
        copy = remote(far.at[j], b2.at[j], s2.at[j], r2.at[j], {"slab": over})
        copy.start()
        second.append(copy)

    key = part[pl.ds(tile, 1), :] // 256 * cap + rank[pl.ds(tile, 1), :]
    slot = lax.broadcasted_iota(jnp.int32, (n_chip * cap, 128), 0)
    send_hot = (slot == key).astype(F32).astype(BF16)
    lane16 = lax.broadcasted_iota(jnp.int32, (128, 16), 1)
    mate = jnp.sum(jnp.where(lane16 == tile, part_t[...], 0), axis=1, keepdims=True)
    mate_tile, mate_row = mate // 128, mate % 128
    lane = lax.broadcasted_iota(jnp.int32, (128, 128), 1)
    low_hot = (lane == mate_row).astype(F32).astype(BF16)
    ranks = lax.dot_general(
        low_hot,
        rank[...].astype(F32).astype(BF16),
        (((1,), (1,)), ((), ())),
        preferred_element_type=F32,
    )
    mate_hot = lane16 == mate_tile
    mate_rank = jnp.sum(jnp.where(mate_hot, ranks, 0.0), axis=1, keepdims=True).astype(jnp.int32)
    mate_irrep = jnp.sum(
        jnp.where(lane == mate_tile, jnp.broadcast_to(irr[0:1, :], (128, 128)), 0.0),
        axis=1,
        keepdims=True,
    )
    source = (mate_tile % 2) * (n_chip * cap) + (mate_tile // 2) * cap + mate_rank
    arrive_hot = (
        (lax.broadcasted_iota(jnp.int32, (128, 2 * n_chip * cap), 1) == source)
        .astype(F32)
        .astype(BF16)
    )

    home.wait_recv()
    third = [[] for _ in chunks]
    fourth = [[] for _ in chunks]

    def relay(i, d):
        block = rows[i].at[core, (chip - d) % n_chip]
        copy = remote(block, block, s4.at[i, d], r4.at[i, d], {"slab": sib})
        copy.start()
        fourth[i].append(copy)

    for i, (lo, hi) in enumerate(chunks):
        for j in range(lo, hi):
            second[j].wait_recv()
            lad[j] = pp[s, j] + b1[1, j] + b2[j]
        for j in range(lo, hi):
            cols = slice((j - lo) * 128, (j - lo + 1) * 128)
            packed = pick(send_hot, lad[j])
            for c in range(n_chip):
                packs[i][c, :, cols] = packed[c * cap : (c + 1) * cap]
        for d in sorted(range(1, n_chip), key=lambda d: -min(d, n_chip - d)):
            other, device = chip_at(d)
            copy = remote(
                packs[i].at[other], rows[i].at[core, chip], s3.at[i, d], r3.at[i, d], device
            )
            copy.start()
            third[i].append((d, copy))
        rows[i][core, chip] = packs[i][chip]
        relay(i, 0)
    for i, (lo, hi) in enumerate(chunks):
        for d, copy in sorted(third[i], key=lambda e: min(e[0], n_chip - e[0])):
            copy.wait_recv()
            relay(i, d)
    for i, (lo, hi) in enumerate(chunks):
        for copy in fourth[i]:
            copy.wait_recv()
        for j in range(lo, hi):
            cols = slice((j - lo) * 128, (j - lo + 1) * 128)
            got = jnp.concatenate(
                [rows[i][c, d, :, cols] for c in range(2) for d in range(n_chip)], axis=0
            )
            yrow[j] = pick(arrive_hot, got)

    mate_out[...] = jnp.broadcast_to(mate_irrep, (128, 128))
    for copy in first + [home] + second:
        copy.wait_send()
    for i in range(n_chunk):
        for _, copy in third[i]:
            copy.wait_send()
        for copy in fourth[i]:
            copy.wait_send()


def combine(n_pair, width, cap, cid, part, part_t, rank, irr, pp):
    n_chip = 2 * n_pair
    dma = pltpu.SemaphoreType.DMA
    chunks = [(0, 3), (3, width)] if width <= W_MORE else [(0, width)]
    wide = [(hi - lo) * 128 for lo, hi in chunks]
    return pl.pallas_call(
        functools.partial(combine_kernel, n_pair, width, cap, chunks),
        out_shape=[jax.ShapeDtypeStruct((width, 128, 128), F32)] * 2
        + [jax.ShapeDtypeStruct((128, 128), F32)],
        in_specs=[vspec()] * 5,
        out_specs=[vspec()] * 3,
        scratch_shapes=[
            pltpu.VMEM((2, width, 128, 128), F32),
            pltpu.VMEM((width, 128, 128), F32),
            pltpu.VMEM((width, 128, 128), F32),
            *[pltpu.VMEM((n_chip, cap, w), F32) for w in wide],
            *[pltpu.VMEM((2, n_chip, cap, w), F32) for w in wide],
            dma((width,)),
            dma((width,)),
            dma,
            dma,
            dma((width,)),
            dma((width,)),
            dma((len(chunks), n_chip)),
            dma((len(chunks), n_chip)),
            dma((len(chunks), n_chip)),
            dma((len(chunks), n_chip)),
        ],
        compiler_params=pltpu.CompilerParams(
            collective_id=cid,
            has_side_effects=True,
            vmem_limit_bytes=VLIM if cap > CAP_FAST else 24 * 1024 * 1024,
        ),
        name=f"combine{cid}",
    )(part, part_t, rank, irr, pp)


def finish_kernel(width, pi, ri, lad, yrow, mate, out):
    own = pi[lax.axis_index("slab")]
    for q in range(12):
        k = ri[q]
        at = jnp.int32(0)
        for q2 in range(q):
            at = at + jnp.where(ri[q2] == k, 1, 0)
        at = jnp.minimum(at, width - 1)
        direct = jnp.where(own == k, lad[at], 0.0)
        swapped = jnp.where(mate[...] == k.astype(F32), yrow[at], 0.0)
        out[:, q * 128 : (q + 1) * 128] = direct + pltpu.roll(swapped, 64, 1)


def finish(width, pi, ri, lad, yrow, mate):
    return pl.pallas_call(
        functools.partial(finish_kernel, width),
        out_shape=jax.ShapeDtypeStruct((128, 1536), F32),
        in_specs=[sspec()] * 2 + [vspec()] * 3,
        out_specs=vspec(),
        compiler_params=pltpu.CompilerParams(vmem_limit_bytes=8 * 1024 * 1024),
        name=f"finish{width}",
    )(pi, ri, lad, yrow, mate)


def shards(n_pair, amplitudes, integrals, pi, cd, ri, partner):
    amp = amplitudes.reshape(4, 128, 128)
    v = integrals.reshape(integrals.shape[1:])
    part = partner.reshape(16, 128)
    part_t = part.T
    t0, t1, rank, irr, branch = gather(n_pair, (0, 1), True, 0, pi, cd, ri, amp, part)

    def rest(width, cap, cid, extra, t0, t1):
        tiles = [t0, t1]
        if extra is not None:
            tiles += gather(n_pair, (2, 3), False, extra, pi, cd, ri, amp, part)
        pp = multiply(width, pi, cd, ri, v, tiles)
        lad, yrow, mate = combine(n_pair, width, cap, cid, part, part_t, rank, irr, pp)
        return finish(width, pi, ri, lad, yrow, mate)

    return lax.switch(
        branch[0],
        [
            functools.partial(rest, W_FAST, CAP_FAST, 1, None),
            functools.partial(rest, W_MORE, CAP_FAST, 6, None),
            functools.partial(rest, W_MORE, CAP_FAST, 2, 3),
            functools.partial(rest, 12, 128, 4, 5),
        ],
        t0,
        t1,
    )


def solution(mesh):
    placed = (P("pair", "slab", "virt"), P("slab", None, "virt"), P("pair"), P(), P("virt"), P())
    return jax.shard_map(
        functools.partial(shards, mesh.shape["pair"]),
        mesh=mesh,
        in_specs=placed,
        out_specs=P(("pair", "slab"), "virt"),
        check_vma=False,
    )
```
